32 devices in a mesh: dp: 4 (over z), seq: 8 (over y, x, core).
Axes of the slice: x: 2, y: 2, z: 4, core: 2. Of those that a mesh axis runs over, the one named last changes fastest.
Arguments:
- tokens: bfloat16 [16, 2048, 768], P('dp', 'seq'), may hold values from -6 to 6
- token_types: int32 [16, 2048], P('dp'), may hold values 0 or 1
- segment_ids: int32 [16, 2048], P('dp'), may hold values from 0 to 7, never falling along the last dimension, each value on 1 to 1024 neighbouring positions
- query_weight: bfloat16 [1536, 1536], P(('dp', 'seq')), may hold values from -0.21875 to 0.21875
- query_bias: bfloat16 [3072], P(('dp', 'seq')), may hold values from -3 to 3
- key_weight: bfloat16 [768, 768], P(('dp', 'seq')), may hold values from -0.21875 to 0.21875
- value_weight: bfloat16 [768, 768], P(('dp', 'seq')), may hold values from -0.21875 to 0.21875
- value_bias: bfloat16 [768], P(('dp', 'seq')), may hold values from -0.29882812 to 0.29882812
- out_weight: bfloat16 [768, 768], P(('dp', 'seq')), may hold values from -1.75 to 1.75
- out_bias: bfloat16 [768], P(('dp', 'seq')), may hold values from -1.1953125 to 1.1953125
- norm1_gain: bfloat16 [768], P(('dp', 'seq')), may hold values from 0.5 to 1.5
- norm1_bias: bfloat16 [768], P(('dp', 'seq')), may hold values from -1.1953125 to 1.1953125
- up_weight: bfloat16 [768, 3072], P(('dp', 'seq')), may hold values from -0.21875 to 0.21875
- up_bias: bfloat16 [3072], P(('dp', 'seq')), may hold values from -1.796875 to 1.796875
- down_weight: bfloat16 [3072, 768], P(('dp', 'seq')), may hold values from -0.109375 to 0.109375
- down_bias: bfloat16 [768], P(('dp', 'seq')), may hold values from -1.1953125 to 1.1953125
- norm2_gain: bfloat16 [768], P(('dp', 'seq')), may hold values from 0.5 to 1.5
- norm2_bias: bfloat16 [768], P(('dp', 'seq')), may hold values from -1.1953125 to 1.1953125
- cotangent: bfloat16 [16, 2048, 768], P('dp', 'seq'), may hold values from -6 to 6
Outputs:
- layer_output: bfloat16 [16, 2048, 768], P('dp', 'seq')
- input_grad: float32 [16, 2048, 768], P('dp', 'seq')
- grad_query_weight: float32 [1536, 1536], P(('dp', 'seq'))
- grad_query_bias: float32 [3072], P(('dp', 'seq'))
- grad_key_weight: float32 [768, 768], P(('dp', 'seq'))
- grad_value_weight: float32 [768, 768], P(('dp', 'seq'))
- grad_value_bias: float32 [768], P(('dp', 'seq'))
- grad_out_weight: float32 [768, 768], P(('dp', 'seq'))
- grad_out_bias: float32 [768], P(('dp', 'seq'))
- grad_norm1_gain: float32 [768], P(('dp', 'seq'))
- grad_norm1_bias: float32 [768], P(('dp', 'seq'))
- grad_up_weight: float32 [768, 3072], P(('dp', 'seq'))
- grad_up_bias: float32 [3072], P(('dp', 'seq'))
- grad_down_weight: float32 [3072, 768], P(('dp', 'seq'))
- grad_down_bias: float32 [768], P(('dp', 'seq'))
- grad_norm2_gain: float32 [768], P(('dp', 'seq'))
- grad_norm2_bias: float32 [768], P(('dp', 'seq'))
The draws below stay inside these ranges and needn't reach their ends.
All inputs are finite; a program needn't handle non-finite values. No bound on the sum of `token_types` on one device may be relied on, other than what follows from the above.
Results may differ from the reference program's by a relative error of at most 0.02.
Values may be sent and summed in bfloat16 or wider, within the bound.
No kernel may reach another device: no remote copies, remote signals or barrier semaphores. Data moves between devices by JAX's collectives and lax.ppermute only.
A program may use at most 256 MiB of HBM per device.

```python
import math
import jax
import jax.numpy as jnp
import numpy as np
from jax import lax

D = 768
HEADS = 12
HEAD_DIM = 64
FF = 3072
LEN = 2048
DOCS = 8
NSEQ = 16


def plant(result, own_key, least, largest):
    longest = result.shape.index(max(result.shape))
    spots = []
    for shift in (0, 1):
        where = [jax.random.randint(jax.random.fold_in(own_key, axis), (), 0, length) for axis, length in enumerate(result.shape)]
        where[longest] = (where[longest] + shift) % result.shape[longest]
        spots.append(tuple(where))
    return result.at[spots[0]].set(least).at[spots[1]].set(largest)


def steps_of(rng, extent, pieces, smallest, high):
    gain, own = 1.0, jax.random.fold_in(rng, 6)
    for dim, shards_of in pieces:
        heights = jnp.exp(jax.random.uniform(jax.random.fold_in(own, dim), (shards_of,), jnp.float32, smallest / len(pieces), high / len(pieces)))
        gain = gain * jnp.repeat(heights, extent[dim] // shards_of).reshape([-1 if axis == dim else 1 for axis in range(len(extent))])
    return gain


def length_profile(count, total, reach, skew):
    portions = [(1 << 20) // math.isqrt(rank ** skew) + 1 for rank in range(2, count + 1)]
    spare, given = total - reach - (count - 1), [1] * (count - 1)
    while spare > 0:
        candidates = [i for i in range(count - 1) if given[i] < reach]
        whole, budget = sum([portions[i] for i in candidates]), spare
        for i in candidates:
            more = min(reach - given[i], max(1, budget * portions[i] // whole), spare)
            given[i] = given[i] + more
            spare = spare - more
    return np.array([reach] + given)


def uneven(key, count, total, bound, slope):
    if count == 2:
        one = jax.random.randint(key, (), max(1, total - bound), min(bound, total - 1) + 1)
        return jnp.stack([one, total - one])
    lengths = jnp.asarray(length_profile(count, total, bound, slope), jnp.int32)
    pairs = (count - 1) // 2
    donor, sink = lengths[1:1 + 2 * pairs:2], lengths[2:2 + 2 * pairs:2]
    room = jnp.minimum(donor - 1, bound - sink)
    moved = jax.random.randint(jax.random.fold_in(key, 1), (pairs,), 0, 1 << 20) % (room + 1)
    lengths = lengths.at[1:1 + 2 * pairs:2].set(donor - moved).at[2:2 + 2 * pairs:2].set(sink + moved)
    return lengths[jax.random.permutation(jax.random.fold_in(key, 2), count)]


def bell_draw(rng, shape, scale, reach, cuts=(), kind=jnp.bfloat16):
    factor_of = steps_of(rng, shape, cuts, -0.22, 0.18) if cuts else 1.0
    drawn = jax.random.normal(rng, shape, jnp.float32) * scale * factor_of
    return jnp.minimum(jnp.maximum(drawn, -reach), reach).astype(kind)


def setup_inputs(seed: int = 0) -> dict:
    streams_of = jax.random.split(jax.random.key(seed), 20)
    tokens = bell_draw(streams_of[0], (NSEQ, LEN, D), 1.0, 6.0, ((0, 4), (1, 8)))
    token_types = plant((jax.random.randint(streams_of[1], (NSEQ, LEN), 0, 4) < 1).astype(jnp.int32), jax.random.fold_in(streams_of[1], 1), 0, 1)
    segment_ids = jax.vmap(lambda own: jnp.searchsorted(jnp.cumsum(uneven(own, DOCS, LEN, LEN // 2, 2)), jnp.arange(LEN), side="right"))(jax.random.split(streams_of[2], NSEQ)).reshape((NSEQ, LEN)).astype(jnp.int32)
    query_weight = bell_draw(streams_of[3], (2 * D, 2 * D), D ** -0.5, 0.21875, ((0, 32),))
    query_bias = bell_draw(streams_of[4], (4 * D,), 0.5, 3.0, ((0, 32),))
    key_weight = bell_draw(streams_of[5], (D, D), D ** -0.5, 0.21875, ((0, 32),))
    value_weight = bell_draw(streams_of[6], (D, D), D ** -0.5, 0.21875, ((0, 32),))
    value_bias = bell_draw(streams_of[7], (D,), 0.05, 0.29882812, ((0, 32),))
    out_weight = bell_draw(streams_of[8], (D, D), (D // 64) ** -0.5, 1.75, ((0, 32),))
    out_bias = bell_draw(streams_of[9], (D,), 0.2, 1.1953125, ((0, 32),))
    norm1_gain = jnp.clip(1.0 + 0.1 * jax.random.normal(streams_of[10], (D,), jnp.float32), 0.5, 1.5).astype(jnp.bfloat16)
    norm1_bias = bell_draw(streams_of[11], (D,), 0.2, 1.1953125, ((0, 32),))
    up_weight = bell_draw(streams_of[12], (D, FF), D ** -0.5, 0.21875, ((0, 32),))
    up_bias = bell_draw(streams_of[13], (FF,), 0.3, 1.796875, ((0, 32),))
    down_weight = bell_draw(streams_of[14], (FF, D), FF ** -0.5, 0.109375, ((0, 32),))
    down_bias = bell_draw(streams_of[15], (D,), 0.2, 1.1953125, ((0, 32),))
    norm2_gain = jnp.clip(1.0 + 0.1 * jax.random.normal(streams_of[16], (D,), jnp.float32), 0.5, 1.5).astype(jnp.bfloat16)
    norm2_bias = bell_draw(streams_of[17], (D,), 0.2, 1.1953125, ((0, 32),))
    cotangent = bell_draw(streams_of[18], (NSEQ, LEN, D), 1.0, 6.0, ((0, 4), (1, 8)))
    return dict(tokens=tokens, token_types=token_types, segment_ids=segment_ids, query_weight=query_weight, query_bias=query_bias, key_weight=key_weight, value_weight=value_weight, value_bias=value_bias, out_weight=out_weight, out_bias=out_bias, norm1_gain=norm1_gain, norm1_bias=norm1_bias, up_weight=up_weight, up_bias=up_bias, down_weight=down_weight, down_bias=down_bias, norm2_gain=norm2_gain, norm2_bias=norm2_bias, cotangent=cotangent)


@jax.custom_vjp
def low(v):
    return lax.optimization_barrier(v.astype(jnp.bfloat16)).astype(jnp.float32)

@jax.custom_vjp
def low_back(v):
    return v

def low_keep(v):
    return (low(v), None)

def low_pass(kept, grad):
    return (grad,)

def back_keep(v):
    return (v, None)

def back_low(kept, grad):
    return (low(grad),)
low.defvjp(low_keep, low_pass)
low_back.defvjp(back_keep, back_low)
NORM_EPS = 1e-12
MASKED = -1e+30

def round_both(tensor):
    return low(low_back(tensor))

def matmul_high(left_op, right_op):
    return jnp.dot(left_op, right_op, precision=lax.Precision.HIGHEST, preferred_element_type=jnp.float32)

def layer_norm(hidden, gain_vec, shift_vec):
    center = hidden - lax.optimization_barrier(jnp.mean(hidden, axis=-1, keepdims=True))
    spread = lax.optimization_barrier(jnp.mean(center * center, axis=-1, keepdims=True))
    return center * lax.rsqrt(spread + NORM_EPS) * gain_vec + shift_vec

def attend_one(packed):
    queries, key_rows, value_rows, segments, kind_rows = packed
    kind_col = kind_rows[:, None, None]
    joined = jnp.concatenate([key_rows * (1.0 - kind_col), key_rows * kind_col], axis=-1)
    raw_scores = jnp.einsum('qhc,khc->hqk', queries, joined, precision=lax.Precision.HIGHEST)
    raw_scores = low_back(raw_scores)
    same_doc = (segments[:, None] == segments[None, :])[None]
    scores = jnp.where(same_doc, raw_scores * (1.0 / math.sqrt(HEAD_DIM)), MASKED)
    row_max = lax.optimization_barrier(jnp.max(scores, axis=-1, keepdims=True))
    exp_terms = jnp.where(same_doc, jnp.exp(scores - row_max), 0.0)
    probs = exp_terms / lax.optimization_barrier(jnp.sum(exp_terms, axis=-1, keepdims=True))
    return jnp.einsum('hqk,khd->qhd', low(probs), value_rows, precision=lax.Precision.HIGHEST)

def forward(inputs, kind_rows, segments, weights):
    w_query, b_query, w_key, w_value, b_value, w_out, b_out, gain_one, shift_one, w_up, b_up, w_down, b_down, gain_two, shift_two = weights
    groups = inputs.shape[0]
    entity = kind_rows[..., None]
    wordish = 1.0 - entity
    stacked = jnp.concatenate([inputs * wordish, inputs * entity], axis=-1)
    query_shift = wordish * b_query[:2 * D] + entity * b_query[2 * D:]
    queries = round_both(matmul_high(stacked, w_query) + query_shift)
    key_rows = round_both(matmul_high(inputs, w_key))
    value_rows = round_both(matmul_high(inputs, w_value) + b_value)
    attended = lax.map(jax.checkpoint(attend_one), (queries.reshape(groups, LEN, HEADS, 2 * HEAD_DIM), key_rows.reshape(groups, LEN, HEADS, HEAD_DIM), value_rows.reshape(groups, LEN, HEADS, HEAD_DIM), segments, kind_rows))
    attended = round_both(attended.reshape(groups, LEN, D))
    first_sum = inputs + low_back(matmul_high(attended, w_out) + b_out)
    normed = layer_norm(first_sum, gain_one, shift_one)
    up_value = low_back(matmul_high(low(normed), w_up) + b_up)
    activated = low(jax.nn.gelu(up_value, approximate=False))
    second_sum = normed + low_back(matmul_high(activated, w_down) + b_down)
    return layer_norm(second_sum, gain_two, shift_two)

def reference(tokens, token_types, segment_ids, query_weight, query_bias, key_weight, value_weight, value_bias, out_weight, out_bias, norm1_gain, norm1_bias, up_weight, up_bias, down_weight, down_bias, norm2_gain, norm2_bias, cotangent):
    params = tuple((weight.astype(jnp.float32) for weight in (query_weight, query_bias, key_weight, value_weight, value_bias, out_weight, out_bias, norm1_gain, norm1_bias, up_weight, up_bias, down_weight, down_bias, norm2_gain, norm2_bias)))
    groups = NSEQ // 2
    token_groups = tokens.reshape(groups, 2, LEN, D)
    kind_groups = token_types.astype(jnp.float32).reshape(groups, 2, LEN)
    segment_groups = segment_ids.reshape(groups, 2, LEN)
    cot_groups = cotangent.reshape(groups, 2, LEN, D)

    def one_group(totals, group_item):
        group_tokens, group_kinds, group_segments, group_cot = group_item

        def run_layer(inputs, weights):
            return forward(inputs, group_kinds, group_segments, weights)
        output, pullback = jax.vjp(run_layer, group_tokens.astype(jnp.float32), params)
        grad_inputs, grad_weights = pullback(group_cot.astype(jnp.float32))
        totals = jax.tree.map(lambda summed, adding: summed + adding, totals, grad_weights)
        return (totals, (output.astype(jnp.bfloat16), grad_inputs))
    zero_grads = jax.tree.map(jnp.zeros_like, params)
    totals, (outputs, grad_tokens) = lax.scan(one_group, zero_grads, (token_groups, kind_groups, segment_groups, cot_groups))
    grad_wq, grad_bq, grad_wk, grad_wv, grad_bv, grad_wo, grad_bo, grad_g1, grad_s1, grad_wu, grad_bu, grad_wd, grad_bd, grad_g2, grad_s2 = totals
    return (outputs.reshape(NSEQ, LEN, D), grad_tokens.reshape(NSEQ, LEN, D), grad_wq, grad_bq, grad_wk, grad_wv, grad_bv, grad_wo, grad_bo, grad_g1, grad_s1, grad_wu, grad_bu, grad_wd, grad_bd, grad_g2, grad_s2)
```

```python
import functools
import math

import jax
import jax.numpy as jnp
from jax import lax
from jax.experimental import pallas as pl
from jax.experimental.pallas import tpu as pltpu
from jax.sharding import Mesh
from jax.sharding import PartitionSpec as P

HEAD_DIM = 64
DOCS = 8
NORM_EPS = 1e-12
FAR = 2.0**50
LOWEST = -3.0e38
LANES = 128
BF16 = jnp.bfloat16
F32 = jnp.float32


def params(*semantics):
    return pltpu.CompilerParams(
        dimension_semantics=semantics, vmem_limit_bytes=60 * 1024 * 1024
    )


def dot_nn(a, b):
    return lax.dot_general(a, b, (((1,), (0,)), ((), ())), preferred_element_type=F32)


def dot_nt(a, b):
    return lax.dot_general(a, b, (((1,), (1,)), ((), ())), preferred_element_type=F32)


def dot_tn(a, b):
    return lax.dot_general(a, b, (((0,), (0,)), ((), ())), preferred_element_type=F32)


def whole(shape):
    zeros = (0,) * len(shape)
    return pl.BlockSpec(shape, lambda *_: zeros, pipeline_mode=pl.Buffered(1))


def rel_start(me, step, parts, size):
    return pl.multiple_of(lax.rem(me + step, parts) * size, size)


def proj_body(parts, own, heads, me_ref, *refs):
    x_refs = refs[:parts]
    kc_ref, kr_ref, wq_ref, wk_ref, wv_ref, bq_ref, bv_ref = refs[parts : parts + 7]
    q_ref, kj_ref, kjt_ref, vx_ref, vt_ref = refs[parts + 7 :]
    me = me_ref[0]
    width = x_refs[0].shape[1]
    for step in range(parts):
        at = rel_start(me, step, parts, own)
        rows = pl.ds(at, own)
        x = x_refs[step][...]
        entity = kc_ref[rows, :] > 0.5
        word_q = dot_nn(x, wq_ref[:width, :]) + bq_ref[0:1, :]
        entity_q = dot_nn(x, wq_ref[width:, :]) + bq_ref[1:2, :]
        queries = jnp.where(entity, entity_q, word_q).astype(BF16)
        q_ref[rows, :] = queries * BF16(1.0 / math.sqrt(HEAD_DIM))
        keys = dot_nn(x, wk_ref[...]).astype(BF16).astype(F32)
        values = (dot_nn(x, wv_ref[...]) + bv_ref[...]).astype(BF16).astype(F32)
        keys_t = keys.T
        values_t = values.T
        row_entity = kr_ref[:, rows] > 0.5
        zero = jnp.zeros((own, HEAD_DIM), F32)
        for head in range(heads):
            part = slice(head * HEAD_DIM, (head + 1) * HEAD_DIM)
            wide = slice(head * LANES, (head + 1) * LANES)
            k = keys[:, part]
            kj_ref[rows, wide] = jnp.concatenate(
                [jnp.where(entity, 0.0, k), jnp.where(entity, k, 0.0)], axis=1
            ).astype(BF16)
            kt = keys_t[part, :]
            kjt_ref[wide, rows] = jnp.concatenate(
                [jnp.where(row_entity, 0.0, kt), jnp.where(row_entity, kt, 0.0)], axis=0
            ).astype(BF16)
            v = values[:, part]
            pair = [v, zero] if head % 2 == 0 else [zero, v]
            vx_ref[rows, wide] = jnp.concatenate(pair, axis=1).astype(BF16)
        vt_ref[:, rows] = values_t.astype(BF16)


def project(me, xs, kind_col, kind_row, wq, wk, wv, bq, bv, groups, own, heads):
    parts = len(xs)
    rows = parts * own
    length = groups * rows
    width = xs[0].shape[1]
    feats = heads * HEAD_DIM
    grid_spec = pltpu.PrefetchScalarGridSpec(
        num_scalar_prefetch=1,
        grid=(groups,),
        in_specs=[pl.BlockSpec((own, width), lambda i, m: (i, 0))] * parts
        + [
            pl.BlockSpec((rows, 1), lambda i, m: (i, 0)),
            pl.BlockSpec((1, rows), lambda i, m: (0, i)),
            whole(wq.shape),
            whole(wk.shape),
            whole(wv.shape),
            whole(bq.shape),
            whole(bv.shape),
        ],
        out_specs=[
            pl.BlockSpec((rows, 2 * feats), lambda i, m: (i, 0)),
            pl.BlockSpec((rows, 2 * feats), lambda i, m: (i, 0)),
            pl.BlockSpec((2 * feats, rows), lambda i, m: (0, i)),
            pl.BlockSpec((rows, 2 * feats), lambda i, m: (i, 0)),
            pl.BlockSpec((feats, rows), lambda i, m: (0, i)),
        ],
    )
    return pl.pallas_call(
        functools.partial(proj_body, parts, own, heads),
        grid_spec=grid_spec,
        out_shape=[
            jax.ShapeDtypeStruct((length, 2 * feats), BF16),
            jax.ShapeDtypeStruct((length, 2 * feats), BF16),
            jax.ShapeDtypeStruct((2 * feats, length), BF16),
            jax.ShapeDtypeStruct((length, 2 * feats), BF16),
            jax.ShapeDtypeStruct((feats, length), BF16),
        ],
        compiler_params=params("arbitrary"),
        name="project",
    )(me, *xs, kind_col, kind_row, wq, wk, wv, bq, bv)


def attend_body(parts, own, heads, me_ref, lo_ref, hi_ref, *refs):
    q_ref, mq_ref, kj_ref, mk_ref, vt_ref = refs[:5]
    out_refs = refs[5 : 5 + parts]
    lse_ref, acc_ref, max_ref, sum_ref = refs[5 + parts :]
    me = me_ref[0]
    group = pl.program_id(0)
    for step in range(parts):
        at = rel_start(me, step, parts, own)
        rows = pl.ds(at, own)
        block = group * parts + lax.rem(me + step, parts)
        acc_ref[...] = jnp.zeros_like(acc_ref)
        max_ref[...] = jnp.full_like(max_ref, LOWEST)
        sum_ref[...] = jnp.zeros_like(sum_ref)

        def fold(kb, carry):
            keys_at = pl.ds(pl.multiple_of(kb * own, own), own)
            key_mark = mk_ref[keys_at, :]
            query_mark = mq_ref[rows, :]
            for head in range(heads):
                wide = slice(head * LANES, (head + 1) * LANES)
                part = slice(head * HEAD_DIM, (head + 1) * HEAD_DIM)
                k = jnp.concatenate([kj_ref[keys_at, wide], key_mark], axis=1)
                q = jnp.concatenate([q_ref[rows, wide], query_mark], axis=1)
                scores = dot_nt(k, q)
                old_max = max_ref[head : head + 1, :]
                new_max = jnp.maximum(old_max, jnp.max(scores, axis=0, keepdims=True))
                factor = jnp.exp(old_max - new_max)
                terms = jnp.exp(scores - new_max)
                sum_ref[head : head + 1, :] = sum_ref[head : head + 1, :] * factor + jnp.sum(
                    terms, axis=0, keepdims=True
                )
                acc_ref[part, :] = acc_ref[part, :] * factor + dot_nn(
                    vt_ref[part, keys_at], terms.astype(BF16)
                )
                max_ref[head : head + 1, :] = new_max
            return carry

        lax.fori_loop(lo_ref[block], hi_ref[block], fold, 0)
        lse_ref[:, rows] = max_ref[...] + jnp.log(sum_ref[...])
        inverse = 1.0 / sum_ref[...]
        for first in range(0, heads, 2):
            last = min(first + 2, heads)
            tall = jnp.concatenate(
                [
                    acc_ref[h * HEAD_DIM : (h + 1) * HEAD_DIM, :] * inverse[h : h + 1, :]
                    for h in range(first, last)
                ],
                axis=0,
            )
            out_refs[step][:, first * HEAD_DIM : last * HEAD_DIM] = tall.T.astype(BF16)


def attend(me, lo, hi, q, mq, kj, mk, vt, groups, parts, own, heads):
    rows = parts * own
    length = groups * rows
    feats = heads * HEAD_DIM
    stats = 8 * ((heads + 7) // 8)
    grid_spec = pltpu.PrefetchScalarGridSpec(
        num_scalar_prefetch=3,
        grid=(groups,),
        in_specs=[
            pl.BlockSpec((rows, 2 * feats), lambda i, *_: (i, 0)),
            pl.BlockSpec((rows, LANES), lambda i, *_: (i, 0)),
            whole(kj.shape),
            whole(mk.shape),
            whole(vt.shape),
        ],
        out_specs=[pl.BlockSpec((own, feats), lambda i, *_: (i, 0))] * parts
        + [pl.BlockSpec((stats, rows), lambda i, *_: (0, i))],
        scratch_shapes=[
            pltpu.VMEM((feats, own), F32),
            pltpu.VMEM((stats, own), F32),
            pltpu.VMEM((stats, own), F32),
        ],
    )
    outs = pl.pallas_call(
        functools.partial(attend_body, parts, own, heads),
        grid_spec=grid_spec,
        out_shape=[jax.ShapeDtypeStruct((groups * own, feats), BF16)] * parts
        + [jax.ShapeDtypeStruct((stats, length), F32)],
        compiler_params=params("arbitrary"),
        name="attend",
    )(me, lo, hi, q, mq, kj, mk, vt)
    return outs[:parts], outs[parts]


def attend_back_body(parts, own, heads, groups, me_ref, lo_ref, hi_ref, *refs):
    q_ref, mq_ref, kj_ref, kjt_ref, vx_ref, mk_ref, kc_ref, lse_ref = refs[:8]
    grad_refs = refs[8 : 8 + parts]
    out_refs = refs[8 + parts : 8 + 2 * parts]
    dq_ref, dk_ref, dv_ref = refs[8 + 2 * parts : 11 + 2 * parts]
    grad_nat, delta_ref, dqt_ref, dk_acc, dv_acc = refs[11 + 2 * parts :]
    me = me_ref[0]
    kb = pl.program_id(0)
    feats = heads * HEAD_DIM
    pairs = (heads + 1) // 2
    stats = delta_ref.shape[0]

    @pl.when(kb == 0)
    def _():
        dqt_ref[...] = jnp.zeros_like(dqt_ref)
        if feats != grad_nat.shape[1]:
            grad_nat[...] = jnp.zeros_like(grad_nat)
        head_row = lax.broadcasted_iota(jnp.int32, (stats, feats), 0)
        head_col = lax.broadcasted_iota(jnp.int32, (stats, feats), 1) // HEAD_DIM
        pick = (head_row == head_col).astype(F32)

        def take(group, carry):
            for step in range(parts):
                source = pl.ds(pl.multiple_of(group * own, own), own)
                at = pl.multiple_of((group * parts + lax.rem(me + step, parts)) * own, own)
                grad = grad_refs[step][source, :]
                grad_nat[pl.ds(at, own), :feats] = grad
                product = grad.astype(F32) * out_refs[step][source, :].astype(F32)
                delta_ref[:, pl.ds(at, own)] = lax.dot_general(
                    pick,
                    product,
                    (((1,), (1,)), ((), ())),
                    precision=lax.Precision.HIGHEST,
                    preferred_element_type=F32,
                )
            return carry

        lax.fori_loop(0, groups, take, 0)

    dk_acc[...] = jnp.zeros_like(dk_acc)
    dv_acc[...] = jnp.zeros_like(dv_acc)
    key_mark = mk_ref[...]

    def fold(qb, carry):
        rows = pl.ds(pl.multiple_of(qb * own, own), own)
        query_mark = mq_ref[rows, :]
        for head in range(heads):
            wide = slice(head * LANES, (head + 1) * LANES)
            pair = slice((head // 2) * LANES, (head // 2 + 1) * LANES)
            query = q_ref[rows, wide]
            k = jnp.concatenate([kj_ref[:, wide], key_mark], axis=1)
            q = jnp.concatenate([query, query_mark], axis=1)
            probs = jnp.exp(dot_nt(k, q) - lse_ref[head : head + 1, rows])
            grad = grad_nat[rows, pair]
            grad_probs = dot_nt(vx_ref[:, wide], grad)
            grad_raw = (probs * (grad_probs - delta_ref[head : head + 1, rows])).astype(BF16)
            dv_acc[:, wide] += dot_nn(probs.astype(BF16), grad)
            dk_acc[:, wide] += dot_nn(grad_raw, query)
            dqt_ref[wide, rows] += dot_nn(kjt_ref[wide, :], grad_raw)
        return carry

    lax.fori_loop(lo_ref[kb], hi_ref[kb], fold, 0)

    entity = kc_ref[...] > 0.5
    for first in range(0, heads, 2):
        grads_k = []
        grads_v = []
        for head in range(first, min(first + 2, heads)):
            base = head * LANES
            word_half = dk_acc[:, base : base + HEAD_DIM]
            entity_half = dk_acc[:, base + HEAD_DIM : base + LANES]
            grads_k.append(jnp.where(entity, entity_half, word_half))
            shift = (head % 2) * HEAD_DIM
            grads_v.append(dv_acc[:, base + shift : base + shift + HEAD_DIM])
        cols = slice(first * HEAD_DIM, first * HEAD_DIM + len(grads_k) * HEAD_DIM)
        dk_ref[:, cols] = jnp.concatenate(grads_k, axis=1).astype(BF16)
        dv_ref[:, cols] = jnp.concatenate(grads_v, axis=1).astype(BF16)

    @pl.when(kb == pl.num_programs(0) - 1)
    def _():
        def turn(qb, carry):
            rows = pl.ds(pl.multiple_of(qb * own, own), own)
            for head in range(heads):
                wide = slice(head * LANES, (head + 1) * LANES)
                tall = dqt_ref[wide, rows] * (1.0 / math.sqrt(HEAD_DIM))
                dq_ref[rows, wide] = tall.T.astype(BF16)
            return carry

        lax.fori_loop(0, pl.num_programs(0), turn, 0)


def attend_back(me, lo, hi, q, mq, kj, kjt, vx, mk, kind_col, lse, grads, outs, own, heads):
    parts = len(grads)
    length = q.shape[0]
    blocks = length // own
    feats = heads * HEAD_DIM
    pairs = (heads + 1) // 2
    stats = lse.shape[0]
    grid_spec = pltpu.PrefetchScalarGridSpec(
        num_scalar_prefetch=3,
        grid=(blocks,),
        in_specs=[
            whole(q.shape),
            whole(mq.shape),
            pl.BlockSpec((own, 2 * feats), lambda i, *_: (i, 0)),
            pl.BlockSpec((2 * feats, own), lambda i, *_: (0, i)),
            pl.BlockSpec((own, 2 * feats), lambda i, *_: (i, 0)),
            pl.BlockSpec((own, LANES), lambda i, *_: (i, 0)),
            pl.BlockSpec((own, 1), lambda i, *_: (i, 0)),
            whole(lse.shape),
        ]
        + [whole(g.shape) for g in grads]
        + [whole(o.shape) for o in outs],
        out_specs=[
            whole(q.shape),
            pl.BlockSpec((own, feats), lambda i, *_: (i, 0)),
            pl.BlockSpec((own, feats), lambda i, *_: (i, 0)),
        ],
        scratch_shapes=[
            pltpu.VMEM((length, pairs * LANES), BF16),
            pltpu.VMEM((stats, length), F32),
            pltpu.VMEM((2 * feats, length), F32),
            pltpu.VMEM((own, 2 * feats), F32),
            pltpu.VMEM((own, 2 * feats), F32),
        ],
    )
    return pl.pallas_call(
        functools.partial(attend_back_body, parts, own, heads, blocks // parts),
        grid_spec=grid_spec,
        out_shape=[
            jax.ShapeDtypeStruct(q.shape, BF16),
            jax.ShapeDtypeStruct((length, feats), BF16),
            jax.ShapeDtypeStruct((length, feats), BF16),
        ],
        compiler_params=params("arbitrary"),
        name="attend_back",
    )(me, lo, hi, q, mq, kj, kjt, vx, mk, kind_col, lse, *grads, *outs)


def norm_stats(value):
    center = value - jnp.mean(value, axis=1, keepdims=True)
    scale = lax.rsqrt(jnp.mean(center * center, axis=1, keepdims=True) + NORM_EPS)
    return center * scale, scale


def norm_back(xhat, scale, grad):
    mean_one = jnp.mean(grad, axis=1, keepdims=True)
    mean_two = jnp.mean(grad * xhat, axis=1, keepdims=True)
    return scale * (grad - mean_one - xhat * mean_two)


def feed_body(parts, feats, me_ref, *refs):
    att_refs = refs[:parts]
    x_ref, ct_ref, wo_ref, wu_ref, wd_ref, bu_ref, vec_ref = refs[parts : parts + 7]
    outs = refs[parts + 7 :]
    out_ref, gf_ref, nat_ref, act_ref, gup_ref, low_ref, g2_ref, g1_ref = outs[:8]
    gatt_refs = outs[8 : 8 + parts]
    su_ref, sv_ref, deriv_ref = outs[8 + parts :]
    me = me_ref[0]
    ff = wu_ref.shape[1]
    chunk = min(768, ff)

    @pl.when(pl.program_id(0) == 0)
    def _():
        su_ref[...] = jnp.zeros_like(su_ref)
        sv_ref[...] = jnp.zeros_like(sv_ref)

    bias_out, gain_one, shift_one = vec_ref[0:1, :], vec_ref[1:2, :], vec_ref[2:3, :]
    bias_down, gain_two, shift_two = vec_ref[3:4, :], vec_ref[4:5, :], vec_ref[5:6, :]
    first_sum = x_ref[...].astype(F32) + bias_out
    for step in range(parts):
        at = rel_start(me, step, parts, feats)
        att = att_refs[step][...]
        for own in range(parts):

            @pl.when(lax.rem(me + step, parts) == own)
            def _(att=att, own=own):
                nat_ref[:, own * feats : (own + 1) * feats] = att

        first_sum = first_sum + dot_nn(att, wo_ref[pl.ds(at, feats), :])
    hat_one, scale_one = norm_stats(first_sum)
    normed = hat_one * gain_one + shift_one
    normed_low = normed.astype(BF16)
    low_ref[...] = normed_low
    second_sum = normed + bias_down
    for at in range(0, ff, chunk):
        cols = slice(at, at + chunk)
        up = dot_nn(normed_low, wu_ref[:, cols]) + bu_ref[:, cols]
        below = 0.5 + 0.5 * lax.erf(up * math.sqrt(0.5))
        density = jnp.exp(-0.5 * up * up) * (1.0 / math.sqrt(2.0 * math.pi))
        deriv_ref[:, cols] = below + up * density
        activated = (up * below).astype(BF16)
        act_ref[:, cols] = activated
        second_sum = second_sum + dot_nn(activated, wd_ref[cols, :])
    hat_two, scale_two = norm_stats(second_sum)
    out_ref[...] = (hat_two * gain_two + shift_two).astype(BF16)
    cotangent = ct_ref[...].astype(F32)
    grad_second = norm_back(hat_two, scale_two, cotangent * gain_two)
    branch_two = grad_second.astype(BF16)
    g2_ref[...] = branch_two
    grad_normed = grad_second
    for at in range(0, ff, chunk):
        cols = slice(at, at + chunk)
        grad_up = (dot_nt(branch_two, wd_ref[cols, :]) * deriv_ref[:, cols]).astype(BF16)
        gup_ref[:, cols] = grad_up
        su_ref[:, cols] += jnp.sum(grad_up.astype(F32), axis=0, keepdims=True)
        grad_normed = grad_normed + dot_nt(grad_up, wu_ref[:, cols])
    grad_first = norm_back(hat_one, scale_one, grad_normed * gain_one)
    gf_ref[...] = grad_first
    branch_one = grad_first.astype(BF16)
    g1_ref[...] = branch_one
    for step in range(parts):
        at = rel_start(me, step, parts, feats)
        gatt_refs[step][...] = dot_nt(branch_one, wo_ref[pl.ds(at, feats), :]).astype(BF16)
    sums = (
        branch_one.astype(F32),
        grad_normed * hat_one,
        grad_normed,
        branch_two.astype(F32),
        cotangent * hat_two,
        cotangent,
    )
    for row, value in enumerate(sums):
        sv_ref[row : row + 1, :] += jnp.sum(value, axis=0, keepdims=True)


def feed(me, atts, x, ct, wo, wu, wd, bias_up, vecs, block):
    parts = len(atts)
    feats = atts[0].shape[1]
    tokens, width = x.shape
    ff = wu.shape[1]
    row = lambda cols: pl.BlockSpec((block, cols), lambda i, m: (i, 0))
    grid_spec = pltpu.PrefetchScalarGridSpec(
        num_scalar_prefetch=1,
        grid=(tokens // block,),
        in_specs=[row(feats)] * parts
        + [row(width), row(width)]
        + [whole(wo.shape), whole(wu.shape), whole(wd.shape), whole(bias_up.shape)]
        + [whole(vecs.shape)],
        out_specs=[row(width), row(width), row(width), row(ff), row(ff)]
        + [row(width), row(width), row(width)]
        + [row(feats)] * parts
        + [whole((1, ff)), whole((8, width))],
        scratch_shapes=[pltpu.VMEM((block, ff), F32)],
    )
    low = lambda cols: jax.ShapeDtypeStruct((tokens, cols), BF16)
    outs = pl.pallas_call(
        functools.partial(feed_body, parts, feats),
        grid_spec=grid_spec,
        out_shape=[
            low(width),
            jax.ShapeDtypeStruct((tokens, width), F32),
            low(width),
            low(ff),
            low(ff),
            low(width),
            low(width),
            low(width),
        ]
        + [low(feats)] * parts
        + [jax.ShapeDtypeStruct((1, ff), F32), jax.ShapeDtypeStruct((8, width), F32)],
        compiler_params=params("arbitrary"),
        name="feed",
    )(me, *atts, x, ct, wo, wu, wd, bias_up, vecs)
    return outs[:8], outs[8 : 8 + parts], outs[8 + parts], outs[9 + parts]


def unproj_body(parts, own, me_ref, *refs):
    x_refs = refs[:parts]
    kc_ref, dq_ref, dk_ref, dv_ref, gf_ref, wq_ref, wk_ref, wv_ref = refs[parts : parts + 8]
    dx_refs = refs[parts + 8 : 2 * parts + 8]
    gq_ref, gk_ref, gv_ref, sq_ref, sv_ref = refs[2 * parts + 8 :]
    me = me_ref[0]
    width = x_refs[0].shape[1]

    @pl.when(pl.program_id(0) == 0)
    def _():
        for ref in (gq_ref, gk_ref, gv_ref, sq_ref, sv_ref):
            ref[...] = jnp.zeros_like(ref)

    for step in range(parts):
        at = rel_start(me, step, parts, own)
        rows = pl.ds(at, own)
        x = x_refs[step][...]
        entity = kc_ref[rows, :] > 0.5
        dq = dq_ref[rows, :]
        dk = dk_ref[rows, :]
        dv = dv_ref[rows, :]
        dq_word = jnp.where(entity, BF16(0), dq)
        dq_entity = jnp.where(entity, dq, BF16(0))
        gq_ref[:width, :] += dot_tn(x, dq_word)
        gq_ref[width:, :] += dot_tn(x, dq_entity)
        gk_ref[...] += dot_tn(x, dk)
        gv_ref[...] += dot_tn(x, dv)
        sq_ref[0:1, :] += jnp.sum(dq_word.astype(F32), axis=0, keepdims=True)
        sq_ref[1:2, :] += jnp.sum(dq_entity.astype(F32), axis=0, keepdims=True)
        sv_ref[...] += jnp.sum(dv.astype(F32), axis=0, keepdims=True)
        dx = (
            dot_nt(dq_word, wq_ref[:width, :])
            + dot_nt(dq_entity, wq_ref[width:, :])
            + dot_nt(dk, wk_ref[...])
            + dot_nt(dv, wv_ref[...])
        )
        if step == 0:
            dx = dx + gf_ref[...]
        dx_refs[step][...] = dx.astype(dx_refs[step].dtype)


def unproject(me, xs, kind_col, dq, dk, dv, gf, wq, wk, wv, groups, own):
    parts = len(xs)
    rows = parts * own
    width = xs[0].shape[1]
    feats = dk.shape[1]
    grid_spec = pltpu.PrefetchScalarGridSpec(
        num_scalar_prefetch=1,
        grid=(groups,),
        in_specs=[pl.BlockSpec((own, width), lambda i, m: (i, 0))] * parts
        + [
            pl.BlockSpec((rows, 1), lambda i, m: (i, 0)),
            pl.BlockSpec((rows, 2 * feats), lambda i, m: (i, 0)),
            pl.BlockSpec((rows, feats), lambda i, m: (i, 0)),
            pl.BlockSpec((rows, feats), lambda i, m: (i, 0)),
            pl.BlockSpec((own, width), lambda i, m: (i, 0)),
            whole(wq.shape),
            whole(wk.shape),
            whole(wv.shape),
        ],
        out_specs=[pl.BlockSpec((own, width), lambda i, m: (i, 0))] * parts
        + [
            whole(wq.shape),
            whole(wk.shape),
            whole(wv.shape),
            whole((2, 2 * feats)),
            whole((1, feats)),
        ],
    )
    outs = pl.pallas_call(
        functools.partial(unproj_body, parts, own),
        grid_spec=grid_spec,
        out_shape=[jax.ShapeDtypeStruct((groups * own, width), F32)]
        + [jax.ShapeDtypeStruct((groups * own, width), BF16)] * (parts - 1)
        + [
            jax.ShapeDtypeStruct(wq.shape, F32),
            jax.ShapeDtypeStruct(wk.shape, F32),
            jax.ShapeDtypeStruct(wv.shape, F32),
            jax.ShapeDtypeStruct((2, 2 * feats), F32),
            jax.ShapeDtypeStruct((1, feats), F32),
        ],
        compiler_params=params("arbitrary"),
        name="unproject",
    )(me, *xs, kind_col, dq, dk, dv, gf, wq, wk, wv)
    return outs[:parts], outs[parts:]


def from_peer(value, step, parts):
    return lax.ppermute(value, "hg", [((i + step) % parts, i) for i in range(parts)])


def split_cols(shard, width):
    return jnp.concatenate(
        [shard[:, at : at + width] for at in range(0, shard.shape[1], width)], axis=0
    )


def join_cols(gathered, rows, blocks):
    devices, _, width = gathered.shape
    return (
        gathered.reshape(devices, blocks, rows, width)
        .transpose(0, 2, 1, 3)
        .reshape(devices * rows, blocks * width)
    )


def per_device(
    tokens,
    token_types,
    segment_ids,
    query_weight,
    query_bias,
    key_weight,
    value_weight,
    value_bias,
    out_weight,
    out_bias,
    norm1_gain,
    norm1_bias,
    up_weight,
    up_bias,
    down_weight,
    down_bias,
    norm2_gain,
    norm2_bias,
    cotangent,
    *,
    devices,
    parts,
):
    groups, own, width = tokens.shape
    length = segment_ids.shape[1]
    all_heads = width // HEAD_DIM
    heads = all_heads // parts
    feats = heads * HEAD_DIM
    ff = up_weight.shape[1]
    everyone = ("dp", "grp", "hg")
    me = lax.axis_index("hg")
    mine = lax.axis_index("grp")
    me_arr = me.reshape(1).astype(jnp.int32)

    q_rows, k_rows = query_weight.shape[0], key_weight.shape[0]
    u_rows, d_rows = up_weight.shape[0], down_weight.shape[0]
    q_blocks, u_blocks = query_weight.shape[1] // width, ff // width
    pack = jnp.concatenate(
        [
            split_cols(query_weight, width),
            key_weight,
            value_weight,
            out_weight,
            split_cols(up_weight, width),
            down_weight,
        ],
        axis=0,
    )
    bundle = lax.all_gather(pack, everyone, axis=0, tiled=False)
    vec_pack = jnp.concatenate(
        [out_bias, norm1_gain, norm1_bias, down_bias, norm2_gain, norm2_bias, value_bias]
        + [query_bias, up_bias]
    ).reshape(1, -1)
    vec_all = lax.all_gather(vec_pack, everyone, axis=0, tiled=True).astype(F32)

    to_groups = lambda v: lax.all_to_all(v, "grp", 0, 0, tiled=True)
    x_mine = to_groups(tokens).reshape(groups * own, width)
    xs = [x_mine] + [from_peer(x_mine, step, parts) for step in range(1, parts)]
    ct = to_groups(cotangent).reshape(groups * own, width)
    kinds = lax.dynamic_index_in_dim(token_types, mine, 0, keepdims=False).astype(F32)
    segs = lax.dynamic_index_in_dim(segment_ids, mine, 0, keepdims=False)
    kind_col = kinds.reshape(length, 1)
    kind_row = kinds.reshape(1, length)
    first_seg = segs[::own]
    last_seg = segs[own - 1 :: own]
    lo = jnp.sum(segs[None, :] < first_seg[:, None], axis=1).astype(jnp.int32) // own
    hi = (
        jnp.sum(segs[None, :] <= last_seg[:, None], axis=1).astype(jnp.int32) + own - 1
    ) // own
    lane = lax.broadcasted_iota(jnp.int32, (length, LANES), 1)
    same = lane == segs[:, None]
    mq = jnp.where(same, FAR, 0.0).astype(BF16)
    mk = jnp.where(same | (lane >= DOCS), 0.0, -FAR).astype(BF16)

    vec_one = vec_all[:, : 7 * k_rows].reshape(devices, 7, k_rows).transpose(1, 0, 2)
    vec_one = vec_one.reshape(7, width)
    vecs = jnp.concatenate([vec_one[:6], jnp.zeros((2, width), F32)], axis=0)
    at = 7 * k_rows
    n_qb, n_ub = query_bias.shape[0], up_bias.shape[0]
    bias_q = vec_all[:, at : at + n_qb].reshape(2, 2 * width)
    bias_up = vec_all[:, at + n_qb : at + n_qb + n_ub].reshape(1, ff)
    bq = lax.dynamic_slice_in_dim(bias_q, me * 2 * feats, 2 * feats, 1)
    bv = lax.dynamic_slice_in_dim(vec_one[6:7], me * feats, feats, 1)

    at = 0
    wq_all = join_cols(bundle[:, at : at + q_blocks * q_rows], q_rows, q_blocks)
    at += q_blocks * q_rows
    wk_all = bundle[:, at : at + k_rows].reshape(width, width)
    at += k_rows
    wv_all = bundle[:, at : at + k_rows].reshape(width, width)
    at += k_rows
    wo = bundle[:, at : at + k_rows].reshape(width, width)
    at += k_rows
    wu = join_cols(bundle[:, at : at + u_blocks * u_rows], u_rows, u_blocks)
    at += u_blocks * u_rows
    wd = bundle[:, at : at + d_rows].reshape(ff, width)
    wq = lax.dynamic_slice_in_dim(wq_all, me * 2 * feats, 2 * feats, 1)
    wk = lax.dynamic_slice_in_dim(wk_all, me * feats, feats, 1)
    wv = lax.dynamic_slice_in_dim(wv_all, me * feats, feats, 1)

    q, kj, kjt, vx, vt = project(
        me_arr, xs, kind_col, kind_row, wq, wk, wv, bq, bv, groups, own, heads
    )
    att_rel, lse = attend(me_arr, lo, hi, q, mq, kj, mk, vt, groups, parts, own, heads)
    atts = [att_rel[0]] + [
        from_peer(att_rel[parts - step], step, parts) for step in range(1, parts)
    ]

    rows, gatt_rel, sum_up, sum_vec = feed(
        me_arr, atts, x_mine, ct, wo, wu, wd, bias_up, vecs, min(256, groups * own)
    )
    out_low, grad_first, att_nat, act, grad_up, normed_low, branch_two, branch_one = rows
    gatts = [gatt_rel[0]] + [
        from_peer(gatt_rel[parts - step], step, parts) for step in range(1, parts)
    ]
    grad_down = dot_tn(act, branch_two).astype(BF16)
    grad_upw = dot_tn(normed_low, grad_up).astype(BF16)
    grad_out = dot_tn(att_nat, branch_one).astype(BF16)
    vec_rows = 8
    feed_vec = jnp.concatenate(
        [
            sum_vec[:6].reshape(6, devices, k_rows).transpose(1, 0, 2).reshape(devices, -1),
            sum_up.reshape(devices, -1),
        ],
        axis=1,
    )
    feed_vec = jnp.pad(feed_vec, ((0, 0), (0, vec_rows * width - feed_vec.shape[1])))
    feed_chunks = jnp.concatenate(
        [
            grad_down.reshape(devices, d_rows, width),
            grad_upw.reshape(devices, u_rows, u_blocks, width)
            .transpose(0, 2, 1, 3)
            .reshape(devices, u_blocks * u_rows, width),
            grad_out.reshape(devices, k_rows, width),
            feed_vec.reshape(devices, vec_rows, width).astype(BF16),
        ],
        axis=1,
    )
    feed_sum = lax.psum_scatter(feed_chunks, everyone, scatter_dimension=0, tiled=False)

    dq, dk, dv = attend_back(
        me_arr, lo, hi, q, mq, kj, kjt, vx, mk, kind_col, lse, gatts, att_rel, own, heads
    )
    dx_rel, (gq, gk, gv, sum_q, sum_v) = unproject(
        me_arr, xs, kind_col, dq, dk, dv, grad_first, wq, wk, wv, groups, own
    )
    dx = dx_rel[0]
    for step in range(1, parts):
        dx = dx + from_peer(dx_rel[parts - step], step, parts).astype(F32)
    input_grad = to_groups(dx.astype(BF16).reshape(groups, own, width)).astype(F32)
    layer_output = to_groups(out_low.reshape(groups, own, width))

    places = devices // parts
    bias_full = jnp.zeros((2, 2 * width), F32)
    bias_full = lax.dynamic_update_slice_in_dim(bias_full, sum_q, me * 2 * feats, 1)
    value_full = jnp.zeros((1, width), F32)
    value_full = lax.dynamic_update_slice_in_dim(value_full, sum_v, me * feats, 1)
    att_vec = jnp.concatenate(
        [bias_full.reshape(devices, -1), value_full.reshape(devices, -1)], axis=1
    )
    wide = 2 * feats
    att_vec = jnp.pad(att_vec, ((0, 0), (0, vec_rows * wide - att_vec.shape[1])))
    att_chunks = jnp.concatenate(
        [
            gq.astype(BF16).reshape(devices, q_rows, wide),
            jnp.concatenate([gk, gv], axis=1).astype(BF16).reshape(devices, k_rows, wide),
            att_vec.reshape(devices, vec_rows, wide).astype(BF16),
        ],
        axis=1,
    )
    chunk_rows = att_chunks.shape[1]
    att_sum = lax.psum_scatter(
        att_chunks.reshape(places, parts * chunk_rows, wide),
        ("dp", "grp"),
        scatter_dimension=0,
        tiled=False,
    ).reshape(parts, chunk_rows, wide)
    by_cols = lax.all_to_all(att_sum, "hg", 0, 0, tiled=True).astype(F32)
    grad_query = by_cols[:, :q_rows].transpose(1, 0, 2).reshape(q_rows, 2 * width)
    kv = by_cols[:, q_rows : q_rows + k_rows]
    grad_key = kv[:, :, :feats].transpose(1, 0, 2).reshape(k_rows, width)
    grad_value = kv[:, :, feats:].transpose(1, 0, 2).reshape(k_rows, width)
    vec_own = jnp.sum(by_cols[:, q_rows + k_rows :], axis=0).reshape(-1)
    grad_query_bias = vec_own[:n_qb]
    grad_value_bias = vec_own[n_qb : n_qb + k_rows]

    feed_sum = feed_sum.astype(F32)
    grad_down_own = feed_sum[:d_rows]
    grad_up_own = jnp.concatenate(
        [
            feed_sum[d_rows + i * u_rows : d_rows + (i + 1) * u_rows]
            for i in range(u_blocks)
        ],
        axis=1,
    )
    at = d_rows + u_blocks * u_rows
    grad_out_own = feed_sum[at : at + k_rows]
    vec_two = feed_sum[at + k_rows :].reshape(-1)
    small = vec_two[: 6 * k_rows].reshape(6, k_rows)
    grad_up_bias = vec_two[6 * k_rows : 6 * k_rows + n_ub]
    return (
        layer_output,
        input_grad,
        grad_query,
        grad_query_bias,
        grad_key,
        grad_value,
        grad_value_bias,
        grad_out_own,
        small[0],
        small[1],
        small[2],
        grad_up_own,
        grad_up_bias,
        grad_down_own,
        small[3],
        small[4],
        small[5],
    )


def solution(mesh):
    dp, seq = mesh.shape["dp"], mesh.shape["seq"]

    def run(tokens, *rest):
        groups = tokens.shape[0] // dp
        parts = seq // groups
        fine = Mesh(mesh.devices.reshape(dp, groups, parts), ("dp", "grp", "hg"))
        block = P("dp", ("grp", "hg"), None)
        shared = P("dp", None)
        mat = P(("dp", "grp", "hg"), None)
        vec = P(("dp", "grp", "hg"))
        in_specs = (block, shared, shared, mat, vec, mat, mat, vec, mat, vec, vec, vec)
        in_specs += (mat, vec, mat, vec, vec, vec, block)
        out_specs = (block, block, mat, vec, mat, mat, vec, mat, vec, vec, vec)
        out_specs += (mat, vec, mat, vec, vec, vec)
        body = functools.partial(per_device, devices=dp * seq, parts=parts)
        return jax.shard_map(
            body, mesh=fine, in_specs=in_specs, out_specs=out_specs, check_vma=False
        )(tokens, *rest)

    return run
```
